32 devices in a mesh: dp: 8 (over z, y), tensor: 4 (over x, core).
Axes of the slice: x: 2, y: 2, z: 4, core: 2. Of those that a mesh axis runs over, the one named last changes fastest.
Arguments:
- tokens: bfloat16 [2048, 2048], P('dp'), may hold values from -6 to 6
- segment_ids: int32 [2048], P('dp'), may hold values from -1 to 3, as said below
- positions: int32 [2048], P('dp'), may hold values from 0 to 255, as said below
- counts: int32 [8], P('dp'), may hold values from 128 to 256, as said below
- query_weight: bfloat16 [2048, 2048], P('dp', 'tensor'), may hold values from -0.125 to 0.125
- key_weight: bfloat16 [2048, 2048], P('dp', 'tensor'), may hold values from -0.125 to 0.125
- value_weight: bfloat16 [2048, 2048], P('dp', 'tensor'), may hold values from -0.125 to 0.125
- output_weight: bfloat16 [2048, 2048], P('tensor', 'dp'), may hold values from -0.75 to 0.75
- attention_gain: bfloat16 [2048], P('dp'), may hold values from 0.5 to 1.5
- gate_weight: bfloat16 [2048, 8192], P('dp', 'tensor'), may hold values from -0.125 to 0.125
- up_weight: bfloat16 [2048, 8192], P('dp', 'tensor'), may hold values from -0.125 to 0.125
- down_weight: bfloat16 [8192, 2048], P('tensor', 'dp'), may hold values from -0.0625 to 0.0625
- forward_gain: bfloat16 [2048], P('dp'), may hold values from 0.5 to 1.5
- cotangent: bfloat16 [2048, 2048], P('dp'), may hold values from -6 to 6
Outputs:
- mixed_out: bfloat16 [2048, 2048], P('dp')
- grad_tokens: float32 [2048, 2048], P('dp')
- grad_query_weight: float32 [2048, 2048], P('dp', 'tensor')
- grad_key_weight: float32 [2048, 2048], P('dp', 'tensor')
- grad_value_weight: float32 [2048, 2048], P('dp', 'tensor')
- grad_output_weight: float32 [2048, 2048], P('tensor', 'dp')
- grad_attention_gain: float32 [2048], P('dp')
- grad_gate_weight: float32 [2048, 8192], P('dp', 'tensor')
- grad_up_weight: float32 [2048, 8192], P('dp', 'tensor')
- grad_down_weight: float32 [8192, 2048], P('tensor', 'dp')
- grad_forward_gain: float32 [2048], P('dp')
The draws below stay inside these ranges and needn't reach their ends.
Inputs may be any that keep to these rules, and one draw needn't show every extreme that they name: `segment_ids`: in each group of 256 slots the first counts slots hold up to four whole sequences one after the other: ids 0, 1, ... never falling, positions counting from 0 within each sequence; the other slots hold id -1. Some group holds a single sequence of 256 tokens. `positions`: positions count from 0 within each sequence; unused slots hold 0. `counts`: some group uses all its slots.
All inputs are finite; a program needn't handle non-finite values.
Results may differ from the reference program's by a relative error of at most 0.013.
Values may be sent and summed in bfloat16 or wider, within the bound.
No kernel may reach another device: no remote copies, remote signals or barrier semaphores. Data moves between devices by JAX's collectives and lax.ppermute only.
A program may use at most 192 MiB of HBM per device.

```python
import math
import jax
import jax.numpy as jnp
from jax import lax

D = 2048
HEADS = 32
HEAD_DIM = 64
FF = 8192
CAP = 256
SLOTS = 2048
N_DP = 8


def token_plan(key):
    devices = SLOTS // CAP
    base_key = jax.random.fold_in(key, 31)
    count_key, full_key, bound_key = jax.random.split(base_key, 3)
    counts = jax.random.randint(count_key, (devices,), CAP // 2, CAP + 1)
    chosen = jax.random.randint(full_key, (), 0, devices)
    device_ids = jnp.arange(devices)
    counts = jnp.where(device_ids == chosen, CAP, counts).astype(jnp.int32)
    boundaries = jax.random.randint(bound_key, (devices, 3), 0, CAP)
    boundaries = 1 + boundaries % jnp.maximum(counts[:, None] - 1, 1)
    boundaries = jnp.where((device_ids == chosen)[:, None], CAP, boundaries)
    places = jnp.arange(CAP)
    before = boundaries[:, :, None] <= places[None, None, :]
    segments = jnp.sum(before.astype(jnp.int32), axis=1)
    starts = jnp.max(jnp.where(before, boundaries[:, :, None], 0), axis=1)
    inside = places[None, :] < counts[:, None]
    segments = jnp.where(inside, segments, -1)
    positions = jnp.where(inside, places[None, :] - starts, 0)
    return (counts, segments.reshape(-1).astype(jnp.int32), positions.reshape(-1).astype(jnp.int32))


def draw_counts(key, part):
    return token_plan(key)[0]


def draw_segment_ids(key, part):
    return token_plan(key)[1]


def draw_positions(key, part):
    return token_plan(key)[2]


def block_scale(own_key, dims, pieces, smallest, largest):
    factor_of, own = 1.0, jax.random.fold_in(own_key, 6)
    for position, parts in pieces:
        draws = jnp.exp(jax.random.uniform(jax.random.fold_in(own, position), (parts,), jnp.float32, smallest / len(pieces), largest / len(pieces)))
        factor_of = factor_of * jnp.repeat(draws, dims[position] // parts).reshape([-1 if axis == position else 1 for axis in range(len(dims))])
    return factor_of


def centred(rng, extent, width, bound, cuts=(), kind=jnp.bfloat16):
    factor_of = block_scale(rng, extent, cuts, -0.22, 0.18) if cuts else 1.0
    result = jax.random.normal(rng, extent, jnp.float32) * width * factor_of
    return jnp.minimum(jnp.maximum(result, -bound), bound).astype(kind)


def setup_inputs(seed: int = 0) -> dict:
    streams_of = jax.random.split(jax.random.key(seed), 15)
    tokens = centred(streams_of[0], (SLOTS, D), 1.0, 6.0, ((0, 8),))
    segment_ids = draw_segment_ids(jax.random.fold_in(streams_of[14], 71), 0)
    positions = draw_positions(jax.random.fold_in(streams_of[14], 71), 0)
    counts = draw_counts(jax.random.fold_in(streams_of[14], 71), 0)
    query_weight = centred(streams_of[4], (D, D), D ** -0.5, 0.125, ((0, 8), (1, 4)))
    key_weight = centred(streams_of[5], (D, D), D ** -0.5, 0.125, ((0, 8), (1, 4)))
    value_weight = centred(streams_of[6], (D, D), D ** -0.5, 0.125, ((0, 8), (1, 4)))
    output_weight = centred(streams_of[7], (D, D), (max(D // 32, 16)) ** -0.5, 0.75, ((0, 4), (1, 8)))
    attention_gain = jnp.clip(1.0 + 0.1 * jax.random.normal(streams_of[8], (D,), jnp.float32), 0.5, 1.5).astype(jnp.bfloat16)
    gate_weight = centred(streams_of[9], (D, FF), D ** -0.5, 0.125, ((0, 8), (1, 4)))
    up_weight = centred(streams_of[10], (D, FF), D ** -0.5, 0.125, ((0, 8), (1, 4)))
    down_weight = centred(streams_of[11], (FF, D), FF ** -0.5, 0.0625, ((0, 4), (1, 8)))
    forward_gain = jnp.clip(1.0 + 0.1 * jax.random.normal(streams_of[12], (D,), jnp.float32), 0.5, 1.5).astype(jnp.bfloat16)
    cotangent = centred(streams_of[13], (SLOTS, D), 1.0, 6.0, ((0, 8),))
    return {"tokens": tokens, "segment_ids": segment_ids, "positions": positions, "counts": counts, "query_weight": query_weight, "key_weight": key_weight, "value_weight": value_weight, "output_weight": output_weight, "attention_gain": attention_gain, "gate_weight": gate_weight, "up_weight": up_weight, "down_weight": down_weight, "forward_gain": forward_gain, "cotangent": cotangent}


EPSILON = 1e-05
ROPE_BASE = 130000.0
MASKED = -1e+30
HIGH = lax.Precision.HIGHEST

@jax.custom_vjp
def low(v):
    return lax.optimization_barrier(v.astype(jnp.bfloat16)).astype(jnp.float32)

@jax.custom_vjp
def low_back(v):
    return v

def low_keep(v):
    return (low(v), None)

def low_pass(kept, grad):
    return (grad,)

def back_keep(v):
    return (v, None)

def back_low(kept, grad):
    return (low(grad),)
low.defvjp(low_keep, low_pass)
low_back.defvjp(back_keep, back_low)

def matmul(left, right):
    return jnp.dot(left, right, preferred_element_type=jnp.float32, precision=HIGH)

def rotary_tables(places):
    half_dim = HEAD_DIM // 2
    inverse = ROPE_BASE ** (-(jnp.arange(half_dim, dtype=jnp.float32) * 2.0 / HEAD_DIM))
    angles = places.astype(jnp.float32)[:, None] * inverse[None, :]
    return (jnp.cos(angles)[:, None, :], jnp.sin(angles)[:, None, :])

def rotate(values, cosine, sine_table):
    half_dim = values.shape[-1] // 2
    front_half = values[..., :half_dim]
    back_half = values[..., half_dim:]
    return jnp.concatenate([front_half * cosine - back_half * sine_table, back_half * cosine + front_half * sine_table], axis=-1)

def rms_scale(stream, gain):
    inverse = lax.rsqrt(lax.optimization_barrier(jnp.mean(stream * stream, axis=1, keepdims=True)) + EPSILON)
    return stream * inverse * gain

def layer(stream, segments, places, token_count, weight_set):
    query_w, key_w, value_w, output_w, gain_one, gate_w, up_w, down_w, gain_two = weight_set
    row_count = stream.shape[0]
    shape_heads = (row_count, HEADS, HEAD_DIM)
    normed = low(rms_scale(stream, gain_one))
    cosine, sine_table = rotary_tables(places)
    queries = low(rotate(low_back(matmul(normed, query_w)).reshape(shape_heads), cosine, sine_table))
    key_rows = low(rotate(low_back(matmul(normed, key_w)).reshape(shape_heads), cosine, sine_table))
    value_rows = low(low_back(matmul(normed, value_w))).reshape(shape_heads)
    scores = jnp.einsum('qhd,khd->hqk', queries, key_rows, precision=HIGH) * (1.0 / math.sqrt(HEAD_DIM))
    scores = low_back(scores)
    allowed = (segments[:, None] == segments[None, :]) & (places[None, :] <= places[:, None])
    scores = jnp.where(allowed[None], scores, MASKED)
    row_top = lax.optimization_barrier(jnp.max(scores, axis=2, keepdims=True))
    exponent = jnp.exp(scores - row_top)
    softmax_weights = exponent / lax.optimization_barrier(jnp.sum(exponent, axis=2, keepdims=True))
    mixed_heads = jnp.einsum('hqk,khd->qhd', low(softmax_weights), value_rows, precision=HIGH).reshape(row_count, HEADS * HEAD_DIM)
    attended = low_back(matmul(low(low_back(mixed_heads)), output_w))
    middle = stream + attended
    normed_two = low(rms_scale(middle, gain_two))
    gate_value = low_back(matmul(normed_two, gate_w))
    up_value = low_back(matmul(normed_two, up_w))
    hidden = low(jax.nn.silu(gate_value) * up_value)
    branch = low_back(matmul(hidden, down_w))
    live_rows = (jnp.arange(row_count, dtype=jnp.int32) < token_count)[:, None]
    return jnp.where(live_rows, middle + branch, 0.0)

def reference(tokens, segment_ids, positions, counts, query_weight, key_weight, value_weight, output_weight, attention_gain, gate_weight, up_weight, down_weight, forward_gain, cotangent):
    weight_set = tuple((element.astype(jnp.float32) for element in (query_weight, key_weight, value_weight, output_weight, attention_gain, gate_weight, up_weight, down_weight, forward_gain)))
    stream = tokens.astype(jnp.float32).reshape(N_DP, CAP, D)
    segments = segment_ids.reshape(N_DP, CAP)
    places = positions.reshape(N_DP, CAP)
    checked = jax.checkpoint(layer)

    def forward(stream_all, weights_now):

        def scan_step(carried, element):
            return (carried, checked(element[0], element[1], element[2], element[3], weights_now))
        unused, outputs = lax.scan(scan_step, jnp.zeros((), jnp.float32), (stream_all, segments, places, counts))
        return outputs
    outputs, pullback = jax.vjp(forward, stream, weight_set)
    grad_stream, grad_set = pullback(cotangent.astype(jnp.float32).reshape(N_DP, CAP, D))
    return (outputs.reshape(SLOTS, D).astype(jnp.bfloat16), grad_stream.reshape(SLOTS, D), grad_set[0], grad_set[1], grad_set[2], grad_set[3], grad_set[4], grad_set[5], grad_set[6], grad_set[7], grad_set[8])
```

```python
import functools
import math

import jax
import jax.numpy as jnp
from jax import lax
from jax.sharding import PartitionSpec as P

HEAD_DIM = 64


EPSILON = 1e-05
ROPE_BASE = 130000.0
MASKED = -1e30


def rotary_tables(positions, head_size):
    half_dim = head_size // 2
    inverse = ROPE_BASE ** (-(jnp.arange(half_dim, dtype=jnp.float32) * 2.0 / head_size))
    angles = positions.astype(jnp.float32)[:, None] * inverse[None, :]
    return (jnp.cos(angles)[:, None, :], jnp.sin(angles)[:, None, :])


def rotate(values, cosine, sine_table):
    half_dim = values.shape[-1] // 2
    front_half = values[..., :half_dim]
    back_half = values[..., half_dim:]
    return jnp.concatenate(
        [
            front_half * cosine - back_half * sine_table,
            back_half * cosine + front_half * sine_table,
        ],
        axis=-1,
    )


def matmul(left, right):
    return jnp.dot(left, right, preferred_element_type=jnp.float32)


def left_product(left, right):
    return lax.dot_general(
        left, right, (((0,), (0,)), ((), ())), preferred_element_type=jnp.float32
    )


def right_product(left, right):
    return lax.dot_general(
        left, right, (((1,), (1,)), ((), ())), preferred_element_type=jnp.float32
    )


def low(value):
    return value.astype(jnp.bfloat16)


def after(value, *earlier):
    return lax.optimization_barrier((value,) + earlier)[0]


class Routes:
    def __init__(self, mesh):
        self.dp = mesh.shape["dp"]
        self.upper = self.dp // 2
        order = list(range(0, self.dp, 2)) + list(range(self.dp - 1, 0, -2))
        self.order = order
        self.place = [order.index(member) for member in range(self.dp)]
        self.onward = [(order[k], order[(k + 1) % self.dp]) for k in range(self.dp)]
        self.backward = [(b, a) for a, b in self.onward]
        self.pair = [(member, member ^ 1) for member in range(self.dp)]
        self.core = [(member, member ^ 1) for member in range(4)]
        self.side = [(member, member ^ 2) for member in range(4)]

    def from_upper(self, step):
        return [
            (2 * u + half, 2 * ((u - step) % self.upper) + half)
            for u in range(self.upper)
            for half in range(2)
        ]


def shards(
    routes,
    tokens,
    segment_ids,
    positions,
    counts,
    query_weight,
    key_weight,
    value_weight,
    output_weight,
    attention_gain,
    gate_weight,
    up_weight,
    down_weight,
    forward_gain,
    cotangent,
):
    rows, width = tokens.shape
    members, upper = routes.dp, routes.upper
    block = query_weight.shape[0]
    head_units = query_weight.shape[1]
    units = gate_weight.shape[1]
    local_units = units // upper
    local_heads = head_units // HEAD_DIM
    quarter = width // 4
    score_scale = 1.0 / math.sqrt(HEAD_DIM)
    me = lax.axis_index("dp")
    my_upper, my_half = me // 2, me % 2
    tensor_index = lax.axis_index("tensor")
    my_side, my_core = tensor_index // 2, tensor_index % 2
    my_quarter = 2 * my_core + my_side
    order = jnp.array(routes.order, jnp.int32)
    my_place = jnp.array(routes.place, jnp.int32)[me]

    def upper_at(step):
        return (my_upper + step) % upper

    def over_dp(value, pairs):
        return lax.ppermute(value, "dp", pairs)

    def over_tensor(value, pairs):
        return lax.ppermute(value, "tensor", pairs)

    def ring_gather(value):
        pieces = [(value, me, 0)]
        ahead, behind = value, value
        for step in range(1, members // 2):
            ahead = over_dp(ahead, routes.onward)
            behind = over_dp(behind, routes.backward)
            pieces.append((ahead, order[(my_place - step) % members], 0))
            pieces.append((behind, order[(my_place + step) % members], 0))
        half = value.shape[0] // 2
        last = order[(my_place + members // 2) % members]
        pieces.append((over_dp(ahead[:half], routes.onward), last, 0))
        pieces.append((over_dp(behind[half:], routes.backward), last, half))
        return pieces

    def assembled(pieces, size):
        whole = jnp.zeros((members * size, pieces[0][0].shape[1]), pieces[0][0].dtype)
        for piece, member, first in pieces:
            whole = lax.dynamic_update_slice_in_dim(whole, piece, member * size + first, 0)
        return whole

    def my_columns(value):
        return lax.dynamic_slice_in_dim(value, my_quarter * quarter, quarter, 1)

    def tensor_gather(value):
        parts = lax.all_gather(value, "tensor", axis=0)
        return jnp.concatenate([parts[0], parts[2], parts[1], parts[3]], axis=1)

    def tensor_scatter(left, right):
        half = width // 2

        def share(core):
            return right_product(left, lax.dynamic_slice_in_dim(right, core * half, half, 0))

        came = over_tensor(low(share(1 - my_core)), routes.core)
        kept = share(my_core) + came.astype(jnp.float32)
        sent = low(lax.dynamic_slice_in_dim(kept, (1 - my_side) * quarter, quarter, 1))
        came = over_tensor(sent, routes.side)
        return lax.dynamic_slice_in_dim(kept, my_side * quarter, quarter, 1) + came.astype(
            jnp.float32
        )

    def upper_gather(value):
        return jnp.concatenate(
            [value] + [over_dp(value, routes.from_upper(step)) for step in range(1, upper)], axis=0
        )

    def upper_scatter(value):
        blocks = value.reshape(upper, rows, -1)
        total = blocks[0]
        for step in range(1, upper):
            total = total + over_dp(low(blocks[step]), routes.from_upper(-step)).astype(jnp.float32)
        return total

    live_rows = (jnp.arange(rows, dtype=jnp.int32) < counts[0])[:, None]
    stream = tokens.astype(jnp.float32)
    cosine, sine_table = rotary_tables(positions, HEAD_DIM)
    shape_heads = (rows, local_heads, HEAD_DIM)
    grad_branch = jnp.where(live_rows, cotangent, jnp.zeros_like(cotangent))

    gains = jnp.stack([attention_gain, forward_gain])
    gains = lax.all_to_all(jnp.broadcast_to(gains[None], (members, 2, block)), "dp", 0, 0)
    gains = gains.transpose(1, 0, 2).reshape(2, width).astype(jnp.float32)
    gain_one, gain_two = gains[0], lax.dynamic_slice_in_dim(gains[1], my_quarter * quarter, quarter)
    projections = jnp.concatenate([query_weight, key_weight, value_weight], axis=1)
    pieces = ring_gather(projections)
    projection_full = assembled(pieces, block)
    output_pieces = ring_gather(after(output_weight.T, pieces[-1][0], pieces[-2][0]))
    output_full = assembled(output_pieces, block)

    def unit_columns(value, step):
        return lax.dynamic_slice_in_dim(value, upper_at(step) * local_units, local_units, 1)

    gate_own, up_own, down_own = after(
        (gate_weight, up_weight, down_weight.T), output_pieces[-1][0], output_pieces[-2][0]
    )
    forward_full = jnp.zeros((upper, 2, block, 3 * local_units), jnp.bfloat16)
    for step in range(upper):
        sent = jnp.concatenate(
            [unit_columns(value, -step) for value in (gate_own, up_own, down_own)], axis=1
        )
        came = over_dp(sent, routes.from_upper(step)) if step else sent
        other = over_dp(came, routes.pair)
        place = upper_at(step)
        forward_full = lax.dynamic_update_slice(forward_full, came[None, None], (place, my_half, 0, 0))
        forward_full = lax.dynamic_update_slice(
            forward_full, other[None, None], (place, 1 - my_half, 0, 0)
        )
    forward_full = forward_full.reshape(width, 3 * local_units)
    gate_up_full, down_full = forward_full[:, : 2 * local_units], forward_full[:, 2 * local_units :]

    inverse_one = lax.rsqrt(jnp.mean(stream * stream, axis=1, keepdims=True) + EPSILON)
    input_one = low(stream * inverse_one * gain_one)
    projected = matmul(input_one, projection_full)
    queries = low(rotate(projected[:, :head_units].reshape(shape_heads), cosine, sine_table))
    key_rows = low(
        rotate(projected[:, head_units : 2 * head_units].reshape(shape_heads), cosine, sine_table)
    )
    value_rows = low(projected[:, 2 * head_units :].reshape(shape_heads))
    allowed = (segment_ids[:, None] == segment_ids[None, :]) & (
        positions[None, :] <= positions[:, None]
    )

    def masked_scores():
        scores = (
            jnp.einsum("qhd,khd->hqk", queries, key_rows, preferred_element_type=jnp.float32)
            * score_scale
        )
        return jnp.where(allowed[None], scores, MASKED)

    scores = masked_scores()
    row_top = jnp.max(scores, axis=2, keepdims=True)
    exponent = jnp.exp(scores - row_top)
    totals = jnp.sum(exponent, axis=2, keepdims=True)
    softmax_weights = low(exponent / totals)
    mixed_flat = low(
        jnp.einsum("hqk,khd->qhd", softmax_weights, value_rows, preferred_element_type=jnp.float32)
    ).reshape(rows, -1)
    log_total = row_top + jnp.log(totals)
    middle = my_columns(stream) + tensor_scatter(mixed_flat, output_full)

    squares = lax.psum(jnp.sum(middle * middle, axis=1), "tensor")
    inverse_two = lax.rsqrt(squares / width + EPSILON)[:, None]
    normed_two = middle * inverse_two
    input_two = tensor_gather(upper_gather(low(normed_two * gain_two)))
    grad_rows = tensor_gather(upper_gather(my_columns(grad_branch)))
    gate_up = matmul(input_two, gate_up_full)
    gate_value, up_value = gate_up[:, :local_units], gate_up[:, local_units:]
    grad_hidden = matmul(grad_rows, down_full)
    sigmoid_gate = jax.nn.sigmoid(gate_value)
    hidden = low(gate_value * sigmoid_gate * up_value)
    grad_gate = low(
        grad_hidden * up_value * sigmoid_gate * (1.0 + gate_value * (1.0 - sigmoid_gate))
    )
    grad_up = low(grad_hidden * gate_value * sigmoid_gate)
    grad_gate_up = jnp.concatenate([grad_gate, grad_up], axis=1)
    grad_normed_two = upper_scatter(tensor_scatter(grad_gate_up, gate_up_full))
    branch = upper_scatter(tensor_scatter(hidden, down_full))
    mixed_out = tensor_gather(low(jnp.where(live_rows, middle + branch, 0.0)))

    grad_forward = jnp.concatenate(
        [left_product(input_two, grad_gate_up), left_product(grad_rows, hidden)], axis=1
    ).reshape(upper, 2, block, 3 * local_units)
    grad_units = [jnp.zeros((block, units), jnp.float32) for _ in range(3)]
    for step in range(upper):
        place = upper_at(step)
        sent = low(lax.dynamic_slice(grad_forward, (place, 1 - my_half, 0, 0), (1, 1, block, 3 * local_units)))
        kept = lax.dynamic_slice(grad_forward, (place, my_half, 0, 0), (1, 1, block, 3 * local_units))
        total = low(kept + over_dp(sent, routes.pair).astype(jnp.float32))[0, 0]
        came = over_dp(total, routes.from_upper(-step)) if step else total
        first = upper_at(-step) * local_units
        for k in range(3):
            grad_units[k] = lax.dynamic_update_slice_in_dim(
                grad_units[k],
                came[:, k * local_units : (k + 1) * local_units].astype(jnp.float32),
                first,
                1,
            )
    grad_gate_weight, grad_up_weight, grad_down_weight = grad_units[0], grad_units[1], grad_units[2].T

    scaled = grad_normed_two * gain_two
    along = lax.psum(jnp.sum(scaled * normed_two, axis=1), "tensor")[:, None] / width
    gain_share_two = jnp.sum(grad_normed_two * normed_two, axis=0)
    grad_middle = my_columns(grad_branch).astype(jnp.float32) + inverse_two * (
        scaled - normed_two * along
    )
    grad_attended = tensor_gather(low(grad_middle))
    grad_mixed = low(matmul(grad_attended, output_full)).reshape(shape_heads)
    softmax_back = jnp.exp(masked_scores() - log_total)
    grad_weights = jnp.einsum(
        "qhd,khd->hqk", grad_mixed, value_rows, preferred_element_type=jnp.float32
    )
    offset = jnp.sum(softmax_back * grad_weights, axis=2, keepdims=True)
    grad_scores = low(softmax_back * (grad_weights - offset))
    grad_query = (
        jnp.einsum("hqk,khd->qhd", grad_scores, key_rows, preferred_element_type=jnp.float32)
        * score_scale
    )
    grad_key = (
        jnp.einsum("hqk,qhd->khd", grad_scores, queries, preferred_element_type=jnp.float32)
        * score_scale
    )
    grad_value = jnp.einsum(
        "hqk,qhd->khd", low(softmax_back), grad_mixed, preferred_element_type=jnp.float32
    )
    grad_projected = jnp.concatenate(
        [
            low(rotate(grad_query, cosine, -sine_table)).reshape(rows, -1),
            low(rotate(grad_key, cosine, -sine_table)).reshape(rows, -1),
            low(grad_value).reshape(rows, -1),
        ],
        axis=1,
    )

    def by_block(value):
        return lax.all_to_all(value, "dp", 1, 0, tiled=True)

    def block_product(left_all, pieces):
        total = None
        for piece, member, first in pieces:
            left = lax.dynamic_slice_in_dim(left_all, member * rows + first, piece.shape[0], 0)
            share = left_product(left, piece)
            total = share if total is None else total + share
        return total

    grad_projections = block_product(by_block(input_one), ring_gather(grad_projected))
    grad_query_weight = grad_projections[:, :head_units]
    grad_key_weight = grad_projections[:, head_units : 2 * head_units]
    grad_value_weight = grad_projections[:, 2 * head_units :]
    grad_output_weight = block_product(by_block(grad_attended), ring_gather(mixed_flat)).T

    grad_normed_one = tensor_scatter(grad_projected, projection_full)
    normed_one = my_columns(stream * inverse_one)
    gain_mine = lax.dynamic_slice_in_dim(gain_one, my_quarter * quarter, quarter)
    scaled = grad_normed_one * gain_mine
    along = lax.psum(jnp.sum(scaled * normed_one, axis=1), "tensor")[:, None] / width
    gain_share_one = jnp.sum(grad_normed_one * normed_one, axis=0)
    grad_tokens = tensor_gather(grad_middle + inverse_one * (scaled - normed_one * along))

    gain_shares = tensor_gather(jnp.stack([gain_share_one, gain_share_two]))
    gain_shares = gain_shares.reshape(2, members, block).transpose(1, 0, 2)
    grad_gains = jnp.sum(lax.all_to_all(gain_shares, "dp", 0, 0), axis=0)
    return (
        mixed_out,
        grad_tokens,
        grad_query_weight,
        grad_key_weight,
        grad_value_weight,
        grad_output_weight,
        grad_gains[0],
        grad_gate_weight,
        grad_up_weight,
        grad_down_weight,
        grad_gains[1],
    )


def solution(mesh):
    return jax.shard_map(
        functools.partial(shards, Routes(mesh)),
        mesh=mesh,
        in_specs=(
            P("dp", None),
            P("dp"),
            P("dp"),
            P("dp"),
            P("dp", "tensor"),
            P("dp", "tensor"),
            P("dp", "tensor"),
            P("tensor", "dp"),
            P("dp"),
            P("dp", "tensor"),
            P("dp", "tensor"),
            P("tensor", "dp"),
            P("dp"),
            P("dp", None),
        ),
        out_specs=(
            P("dp", None),
            P("dp", None),
            P("dp", "tensor"),
            P("dp", "tensor"),
            P("dp", "tensor"),
            P("tensor", "dp"),
            P("dp"),
            P("dp", "tensor"),
            P("dp", "tensor"),
            P("tensor", "dp"),
            P("dp"),
        ),
        check_vma=False,
    )
```

```python
import functools
import math

import jax
import jax.numpy as jnp
from jax import lax
from jax.experimental import pallas as pl
from jax.experimental.pallas import tpu as pltpu
from jax.sharding import PartitionSpec as P


HEAD_DIM = 64


EPSILON = 1e-05
ROPE_BASE = 130000.0
MASKED = -1e30


def rotary_tables(positions, heads):
    half_dim = HEAD_DIM // 2
    inverse = ROPE_BASE ** (-(jnp.arange(half_dim, dtype=jnp.float32) * 2.0 / HEAD_DIM))
    angles = positions.astype(jnp.float32)[:, None] * inverse[None, :]
    cosine, sine = jnp.cos(angles), jnp.sin(angles)
    return (
        jnp.tile(jnp.concatenate([cosine, cosine], axis=1), (1, heads)),
        jnp.tile(jnp.concatenate([-sine, sine], axis=1), (1, heads)),
    )


def rotate(values, cosine, sine):
    half_dim = HEAD_DIM // 2
    size = values.shape[1]
    lane = lax.broadcasted_iota(jnp.int32, values.shape, 1)
    swapped = jnp.where(
        lane % HEAD_DIM < half_dim,
        pltpu.roll(values, size - half_dim, 1),
        pltpu.roll(values, half_dim, 1),
    )
    return values * cosine + swapped * sine


def allowed_pairs(segment_column, segment_row, position_column, position_row):
    return (segment_column[...] == segment_row[...]) & (position_row[...] <= position_column[...])


def attention_forward_kernel(
    inputs,
    weights,
    cosine,
    sine,
    segment_column,
    segment_row,
    position_column,
    position_row,
    projected,
    mixed,
    log_total,
):
    size = mixed.shape[1]
    for part in range(3):
        values = matmul(inputs[...], weights[:, part * size : (part + 1) * size])
        if part < 2:
            values = rotate(values, cosine[...], sine[...])
        projected[:, part * size : (part + 1) * size] = low(values)
    allowed = allowed_pairs(segment_column, segment_row, position_column, position_row)
    for head in range(size // HEAD_DIM):
        first = head * HEAD_DIM
        queries = projected[:, first : first + HEAD_DIM]
        keys = projected[:, size + first : size + first + HEAD_DIM]
        values = projected[:, 2 * size + first : 2 * size + first + HEAD_DIM]
        scores = right_product(queries, keys) * (1.0 / math.sqrt(HEAD_DIM))
        scores = jnp.where(allowed, scores, MASKED)
        top = jnp.max(scores, axis=1, keepdims=True)
        exponent = jnp.exp(scores - top)
        total = jnp.sum(exponent, axis=1, keepdims=True)
        mixed[:, first : first + HEAD_DIM] = low(matmul(low(exponent / total), values))
        log_total[:, head : head + 1] = top + jnp.log(total)


def attention_backward_kernel(
    grad_attended,
    weights,
    projected,
    log_total,
    cosine,
    sine,
    segment_column,
    segment_row,
    position_column,
    position_row,
    grad_projected,
    grad_mixed,
    grad_rotated,
):
    size = weights.shape[1]
    grad_mixed[...] = low(matmul(grad_attended[...], weights[...]))
    allowed = allowed_pairs(segment_column, segment_row, position_column, position_row)
    scale = 1.0 / math.sqrt(HEAD_DIM)
    for head in range(size // HEAD_DIM):
        first = head * HEAD_DIM
        queries = projected[:, first : first + HEAD_DIM]
        keys = projected[:, size + first : size + first + HEAD_DIM]
        values = projected[:, 2 * size + first : 2 * size + first + HEAD_DIM]
        grads = grad_mixed[:, first : first + HEAD_DIM]
        scores = jnp.where(allowed, right_product(queries, keys) * scale, MASKED)
        softmax = jnp.exp(scores - log_total[:, head : head + 1])
        grad_weights = right_product(grads, values)
        offset = jnp.sum(softmax * grad_weights, axis=1, keepdims=True)
        grad_scores = low(softmax * (grad_weights - offset))
        grad_rotated[:, first : first + HEAD_DIM] = matmul(grad_scores, keys) * scale
        grad_rotated[:, size + first : size + first + HEAD_DIM] = (
            left_product(grad_scores, queries) * scale
        )
        grad_projected[:, 2 * size + first : 2 * size + first + HEAD_DIM] = low(
            left_product(low(softmax), grads)
        )
    for part in range(2):
        values = rotate(grad_rotated[:, part * size : (part + 1) * size], cosine[...], -sine[...])
        grad_projected[:, part * size : (part + 1) * size] = low(values)


def attention_forward(inputs, weights, *tables):
    rows, size = inputs.shape[0], weights.shape[1] // 3
    return pl.pallas_call(
        attention_forward_kernel,
        out_shape=(
            jax.ShapeDtypeStruct((rows, 3 * size), jnp.bfloat16),
            jax.ShapeDtypeStruct((rows, size), jnp.bfloat16),
            jax.ShapeDtypeStruct((rows, size // HEAD_DIM), jnp.float32),
        ),
        name="attention_forward",
    )(inputs, weights, *tables)


def attention_backward(grad_attended, weights, projected, log_total, *tables):
    rows, size = grad_attended.shape[0], weights.shape[1]
    return pl.pallas_call(
        attention_backward_kernel,
        out_shape=jax.ShapeDtypeStruct((rows, 3 * size), jnp.bfloat16),
        scratch_shapes=[
            pltpu.VMEM((rows, size), jnp.bfloat16),
            pltpu.VMEM((rows, 2 * size), jnp.float32),
        ],
        name="attention_backward",
    )(grad_attended, weights, projected, log_total, *tables)


def matmul(left, right):
    return jnp.dot(left, right, preferred_element_type=jnp.float32)


def left_product(left, right):
    return lax.dot_general(
        left, right, (((0,), (0,)), ((), ())), preferred_element_type=jnp.float32
    )


def right_product(left, right):
    return lax.dot_general(
        left, right, (((1,), (1,)), ((), ())), preferred_element_type=jnp.float32
    )


def low(value):
    return value.astype(jnp.bfloat16)


def after(value, *earlier):
    return lax.optimization_barrier((value,) + earlier)[0]


def feed_forward_kernel(
    core, inputs, grads, gate_up, down, grad_gate_up, hidden, sent, kept
):
    units, quarter = hidden.shape[1], inputs.shape[2]
    values, grad_hidden = None, None
    for k in range(4):
        part = slice(k * quarter, (k + 1) * quarter)
        value = matmul(inputs[k], gate_up[part, :])
        values = value if k == 0 else values + value
        value = matmul(grads[k], down[part, :])
        grad_hidden = value if k == 0 else grad_hidden + value
    gate, up = values[:, :units], values[:, units:]
    sigmoid = jax.nn.sigmoid(gate)
    hidden[...] = low(gate * sigmoid * up)
    grad_gate_up[:, :units] = low(
        grad_hidden * up * sigmoid * (1.0 + gate * (1.0 - sigmoid))
    )
    grad_gate_up[:, units:] = low(grad_hidden * gate * sigmoid)
    for side in range(2):
        columns = slice(side * quarter, (side + 1) * quarter)
        mine = pl.ds((2 * side + core[0]) * quarter, quarter)
        other = pl.ds((2 * side + 1 - core[0]) * quarter, quarter)
        sent[:, columns] = low(right_product(grad_gate_up[...], gate_up[other, :]))
        kept[:, columns] = right_product(grad_gate_up[...], gate_up[mine, :])


def feed_forward(core, inputs, grads, gate_up, down):
    _, rows, quarter = inputs.shape
    units = down.shape[1]
    tile = 256
    grid = pltpu.PrefetchScalarGridSpec(
        num_scalar_prefetch=1,
        grid=(rows // tile,),
        in_specs=[
            pl.BlockSpec((4, tile, quarter), lambda i, core: (0, i, 0)),
            pl.BlockSpec((4, tile, quarter), lambda i, core: (0, i, 0)),
            pl.BlockSpec((4 * quarter, 2 * units), lambda i, core: (0, 0)),
            pl.BlockSpec((4 * quarter, units), lambda i, core: (0, 0)),
        ],
        out_specs=[
            pl.BlockSpec((tile, 2 * units), lambda i, core: (i, 0)),
            pl.BlockSpec((tile, units), lambda i, core: (i, 0)),
            pl.BlockSpec((tile, 2 * quarter), lambda i, core: (i, 0)),
            pl.BlockSpec((tile, 2 * quarter), lambda i, core: (i, 0)),
        ],
    )
    return pl.pallas_call(
        feed_forward_kernel,
        grid_spec=grid,
        out_shape=(
            jax.ShapeDtypeStruct((rows, 2 * units), jnp.bfloat16),
            jax.ShapeDtypeStruct((rows, units), jnp.bfloat16),
            jax.ShapeDtypeStruct((rows, 2 * quarter), jnp.bfloat16),
            jax.ShapeDtypeStruct((rows, 2 * quarter), jnp.float32),
        ),
        name="feed_forward",
    )(core, inputs, grads, gate_up, down)


class Routes:
    def __init__(self, mesh):
        self.dp = mesh.shape["dp"]
        self.upper = self.dp // 2
        order = list(range(0, self.dp, 2)) + list(range(self.dp - 1, 0, -2))
        self.order = order
        self.place = [order.index(member) for member in range(self.dp)]
        self.onward = [(order[k], order[(k + 1) % self.dp]) for k in range(self.dp)]
        self.backward = [(b, a) for a, b in self.onward]
        self.pair = [(member, member ^ 1) for member in range(self.dp)]
        self.core = [(member, member ^ 1) for member in range(4)]
        self.side = [(member, member ^ 2) for member in range(4)]
        self.uppers = [list(range(half, self.dp, 2)) for half in range(2)]

    def from_upper(self, step):
        return [
            (2 * u + half, 2 * ((u - step) % self.upper) + half)
            for u in range(self.upper)
            for half in range(2)
        ]


def shards(
    routes,
    tokens,
    segment_ids,
    positions,
    counts,
    query_weight,
    key_weight,
    value_weight,
    output_weight,
    attention_gain,
    gate_weight,
    up_weight,
    down_weight,
    forward_gain,
    cotangent,
):
    rows, width = tokens.shape
    members, upper = routes.dp, routes.upper
    block = query_weight.shape[0]
    head_units = query_weight.shape[1]
    units = gate_weight.shape[1]
    local_units = units // upper
    quarter = width // 4
    me = lax.axis_index("dp")
    my_upper, my_half = me // 2, me % 2
    my_quarter = lax.axis_index("tensor")
    my_side, my_core = my_quarter // 2, my_quarter % 2
    order = jnp.array(routes.order, jnp.int32)
    my_place = jnp.array(routes.place, jnp.int32)[me]

    def upper_at(step):
        return (my_upper + step) % upper

    def member_at(step):
        return order[(my_place + step) % members]

    def over_dp(value, pairs):
        return lax.ppermute(value, "dp", pairs)

    def over_tensor(value, pairs):
        return lax.ppermute(value, "tensor", pairs)

    def ring_gather(value, split):
        pieces = [(value, 0, 0)]
        ahead, behind = value, value
        for step in range(1, members // 2):
            ahead = over_dp(ahead, routes.onward)
            behind = over_dp(behind, routes.backward)
            pieces.append((ahead, -step, 0))
            pieces.append((behind, step, 0))
        last = members // 2
        pieces.append((over_dp(ahead[:split], routes.onward), last, 0))
        pieces.append((over_dp(behind[split:], routes.backward), last, split))
        return pieces

    def block_product(left, pieces):
        total = None
        for piece, step, first in pieces:
            begin = member_at(step) * rows + first
            share = left_product(lax.dynamic_slice_in_dim(left, begin, piece.shape[0], 0), piece)
            total = share if total is None else total + share
        return total

    def my_columns(value):
        return lax.dynamic_slice_in_dim(value, my_quarter * quarter, quarter, 1)

    def tensor_parts(value):
        return lax.all_gather(value, "tensor", axis=0)

    def whole_rows(parts):
        return jnp.concatenate([parts[member] for member in range(4)], axis=1)

    def rows_gather(value):
        other = over_tensor(value, routes.side)
        sides = jnp.stack([value, other], axis=1)
        sides = jnp.where(my_side == 0, sides, sides[:, ::-1])[:, :, None]
        other = over_tensor(sides, routes.core)
        both = jnp.concatenate([sides, other], axis=2)
        return jnp.where(my_core == 0, both, both[:, :, ::-1]).reshape(rows, width)

    def tensor_scatter(sent, kept):
        came = over_tensor(sent, routes.core)
        kept = kept + came.astype(jnp.float32)
        sent = low(lax.dynamic_slice_in_dim(kept, (1 - my_side) * quarter, quarter, 1))
        came = over_tensor(sent, routes.side)
        kept = lax.dynamic_slice_in_dim(kept, my_side * quarter, quarter, 1)
        return kept + came.astype(jnp.float32), sent

    def rows_scatter(value):
        parts = value.reshape(rows, 2, 2, quarter)

        def share(core):
            return lax.dynamic_index_in_dim(parts, core, 2, False).reshape(rows, 2 * quarter)

        return tensor_scatter(low(share(1 - my_core)), share(my_core))[0]

    def upper_gather(value):
        return lax.all_gather(
            value, "dp", axis=0, tiled=True, axis_index_groups=routes.uppers
        )

    def upper_scatter(value):
        total = lax.dynamic_slice_in_dim(value, my_upper * rows, rows, 0)
        for step in range(1, upper):
            sent = low(lax.dynamic_slice_in_dim(value, upper_at(step) * rows, rows, 0))
            came = over_dp(sent, routes.from_upper(-step))
            total = total + came.astype(jnp.float32)
        return total

    gain_rows = jnp.concatenate([attention_gain[None], forward_gain[None]], axis=0)
    gain_rows = jnp.pad(gain_rows, ((0, 14), (0, 4 * head_units - block)))
    projections = [query_weight, key_weight, value_weight, output_weight.T]
    projections = jnp.concatenate(projections, axis=1)
    pieces = ring_gather(jnp.concatenate([projections, gain_rows], axis=0), block // 2)
    projection_full = jnp.zeros((width, 3 * head_units), jnp.bfloat16)
    output_full = jnp.zeros((width, head_units), jnp.bfloat16)
    gains = jnp.zeros((2, width), jnp.bfloat16)
    for piece, step, first in pieces:
        start = member_at(step) * block
        projection_full = lax.dynamic_update_slice_in_dim(
            projection_full, piece[: block - first, : 3 * head_units], start + first, 0
        )
        output_full = lax.dynamic_update_slice_in_dim(
            output_full, piece[: block - first, 3 * head_units :], start + first, 0
        )
        if piece.shape[0] + first > block:
            gains = lax.dynamic_update_slice_in_dim(
                gains, piece[block - first : block - first + 2, :block], start, 1
            )
    gains = gains.astype(jnp.float32)
    gain_one, gain_two = gains[0], lax.dynamic_slice_in_dim(gains[1], my_quarter * quarter, quarter)

    live_rows = (jnp.arange(rows, dtype=jnp.int32) < counts[0])[:, None]
    stream = tokens.astype(jnp.float32)
    tables = rotary_tables(positions, head_units // HEAD_DIM) + (
        segment_ids[:, None],
        segment_ids[None, :],
        positions[:, None],
        positions[None, :],
    )
    grad_branch = jnp.where(live_rows, cotangent, jnp.zeros_like(cotangent))
    grad_rows = upper_gather(my_columns(grad_branch))
    grad_parts = tensor_parts(grad_rows)

    def unit_columns(value, step):
        return lax.dynamic_slice_in_dim(value, upper_at(step) * local_units, local_units, 1)

    def units_gather(values):
        columns = len(values) * local_units
        whole = jnp.zeros((upper, 2, block, columns), jnp.bfloat16)
        for step in range(upper):
            sent = [unit_columns(value, -step) for value in values]
            sent = jnp.concatenate(sent, axis=1) if len(sent) > 1 else sent[0]
            came = over_dp(sent, routes.from_upper(step)) if step else sent
            other = over_dp(came, routes.pair)
            for half, value in ((my_half, came), (1 - my_half, other)):
                start = (upper_at(step), half, 0, 0)
                whole = lax.dynamic_update_slice(whole, value[None, None], start)
        return whole.reshape(width, columns)

    gate_own, up_own, down_own = after(
        (gate_weight, up_weight, down_weight.T), pieces[-1][0], pieces[-2][0]
    )
    gate_up_full = units_gather((gate_own, up_own))
    down_full = units_gather((down_own,))

    inverse_one = lax.rsqrt(jnp.mean(stream * stream, axis=1, keepdims=True) + EPSILON)
    input_one = low(stream * inverse_one * gain_one)
    projected, mixed, log_total = attention_forward(input_one, projection_full, *tables)
    middle = my_columns(stream) + rows_scatter(right_product(mixed, output_full))

    squares = lax.psum(jnp.sum(middle * middle, axis=1), "tensor")
    inverse_two = lax.rsqrt(squares / width + EPSILON)[:, None]
    normed_two = middle * inverse_two
    input_two = upper_gather(low(normed_two * gain_two))
    input_parts = tensor_parts(input_two)
    left_one = lax.all_to_all(after(input_one, down_full), "dp", 1, 0, tiled=True)
    grad_gate_up, hidden, sent_two, kept_two = feed_forward(
        my_core[None], input_parts, grad_parts, gate_up_full, down_full
    )
    partial_two, sent_two = tensor_scatter(sent_two, kept_two)
    grad_normed_two = upper_scatter(partial_two)

    later_gate_up, later_hidden = after((grad_gate_up, hidden), sent_two)
    input_two, grad_rows = whole_rows(input_parts), whole_rows(grad_parts)

    def unit_gradient(left, right):
        grads = left_product(left, right).reshape(upper, 2, block, right.shape[1])
        sent = low(lax.dynamic_index_in_dim(grads, 1 - my_half, 1, False))
        came = over_dp(sent, routes.pair).astype(jnp.float32)
        total = low(lax.dynamic_index_in_dim(grads, my_half, 1, False) + came)
        for step in range(upper):
            piece = lax.dynamic_index_in_dim(total, upper_at(step), 0, False)
            if step:
                piece = over_dp(piece, routes.from_upper(-step))
            yield piece.astype(jnp.float32), upper_at(-step) * local_units

    grad_down_weight = jnp.zeros((units, block), jnp.float32)
    for piece, first in unit_gradient(grad_rows, later_hidden):
        grad_down_weight = lax.dynamic_update_slice_in_dim(grad_down_weight, piece.T, first, 0)
    grad_units = []
    for k in range(2):
        grads = jnp.zeros((block, units), jnp.float32)
        right = later_gate_up[:, k * local_units : (k + 1) * local_units]
        for piece, first in unit_gradient(input_two, right):
            grads = lax.dynamic_update_slice_in_dim(grads, piece, first, 1)
        grad_units.append(grads)
    grad_gate_weight, grad_up_weight = grad_units

    scaled = grad_normed_two * gain_two
    along = jnp.sum(scaled * normed_two, axis=1)
    along = lax.psum(along, "tensor")[:, None] / width
    gain_share_two = jnp.sum(grad_normed_two * normed_two, axis=0)
    grad_middle = my_columns(grad_branch).astype(jnp.float32) + inverse_two * (
        scaled - normed_two * along
    )
    grad_attended = rows_gather(low(grad_middle))
    branch = right_product(later_hidden, down_full)
    branch = low(branch)
    branch = lax.psum_scatter(branch, "tensor", scatter_dimension=1, tiled=True)
    branch = lax.psum_scatter(
        branch, "dp", scatter_dimension=0, tiled=True, axis_index_groups=routes.uppers
    )
    grad_projected = attention_backward(grad_attended, output_full, projected, log_total, *tables)

    grad_output = low(left_product(grad_attended, mixed))
    grad_output = lax.psum_scatter(grad_output, "dp", scatter_dimension=0, tiled=True)
    grad_pieces = ring_gather(grad_projected, rows // 2)
    grad_output, branch = after((grad_output, branch), grad_pieces[-1][0], grad_pieces[-2][0])
    grad_output_weight = grad_output.T.astype(jnp.float32)
    mixed_out = low(jnp.where(live_rows, middle + branch.astype(jnp.float32), 0.0))
    mixed_out = rows_gather(mixed_out)
    grad_projections = block_product(left_one, grad_pieces)
    grad_query_weight = grad_projections[:, :head_units]
    grad_key_weight = grad_projections[:, head_units : 2 * head_units]
    grad_value_weight = grad_projections[:, 2 * head_units :]

    grad_normed_one = rows_scatter(right_product(grad_projected, projection_full))
    normed_one = my_columns(stream * inverse_one)
    gain_mine = lax.dynamic_slice_in_dim(gain_one, my_quarter * quarter, quarter)
    scaled = grad_normed_one * gain_mine
    along = lax.psum(jnp.sum(scaled * normed_one, axis=1), "tensor")[:, None] / width
    gain_share_one = jnp.sum(grad_normed_one * normed_one, axis=0)
    grad_tokens = grad_middle + inverse_one * (scaled - normed_one * along)
    grad_tokens = rows_gather(grad_tokens)

    gain_shares = tensor_parts(jnp.stack([gain_share_one, gain_share_two]))
    gain_shares = whole_rows(gain_shares)
    gain_shares = gain_shares.reshape(2, members, block).transpose(1, 0, 2)
    gain_shares = lax.all_to_all(gain_shares, "dp", 0, 0)
    grad_gains = jnp.sum(gain_shares, axis=0)
    return (
        mixed_out,
        grad_tokens,
        grad_query_weight,
        grad_key_weight,
        grad_value_weight,
        grad_output_weight,
        grad_gains[0],
        grad_gate_weight,
        grad_up_weight,
        grad_down_weight,
        grad_gains[1],
    )


def layer(routes, *args):
    return shards(routes, *args)


def solution(mesh):
    routes = Routes(mesh)
    return jax.shard_map(
        functools.partial(layer, routes),
        mesh=mesh,        in_specs=(
            P("dp", None),
            P("dp"),
            P("dp"),
            P("dp"),
            P("dp", "tensor"),
            P("dp", "tensor"),
            P("dp", "tensor"),
            P("tensor", "dp"),
            P("dp"),
            P("dp", "tensor"),
            P("dp", "tensor"),
            P("tensor", "dp"),
            P("dp"),
            P("dp", None),
        ),
        out_specs=(
            P("dp", None),
            P("dp", None),
            P("dp", "tensor"),
            P("dp", "tensor"),
            P("dp", "tensor"),
            P("tensor", "dp"),
            P("dp"),
            P("dp", "tensor"),
            P("dp", "tensor"),
            P("tensor", "dp"),
            P("dp"),
        ),
        check_vma=False,
    )
```
